32 devices in a mesh: src: 4 (over y, x), tgt: 8 (over z, core).
Axes of the slice: x: 2, y: 2, z: 4, core: 2. Of those that a mesh axis runs over, the one named last changes fastest.
Arguments:
- source_values: float32 [16, 65536], P(None, ('src', 'tgt')), may hold values from -6 to 6
- source_phase: float32 [65536], P(('src', 'tgt')), may hold values from -3.140625 to 3.140625
- leaf_interp: bfloat16 [64, 64], replicated, may hold values from -0.75 to 0.75
- level_interp: bfloat16 [11, 2, 64, 64], replicated, may hold values from -0.5 to 0.5
- level_phase: float32 [11, 3, 1024, 64], P(None, None, ('src', 'tgt')), may hold values from -3.140625 to 3.140625
- middle_interp: bfloat16 [64, 64], replicated, may hold values from -0.75 to 0.75
- middle_phase: float32 [2, 1024, 64], P(None, ('src', 'tgt')), may hold values from -3.140625 to 3.140625
- final_phase: float32 [1024, 64], P(('src', 'tgt')), may hold values from -3.140625 to 3.140625
- final_interp: bfloat16 [64, 64], replicated, may hold values from -0.75 to 0.75
- target_phase: float32 [65536], P(('src', 'tgt')), may hold values from -3.140625 to 3.140625
Outputs:
- target_values: float32 [2, 16, 65536], P(None, None, ('src', 'tgt'))
The draws below stay inside these ranges and needn't reach their ends.
All inputs are finite; a program needn't handle non-finite values.
Results may differ from the reference program's by a relative error of at most 0.024.
Values may be sent and summed in bfloat16 or wider, within the bound.
A program may use at most 64 MiB of HBM per device.

```python
import jax
import jax.numpy as jnp

RANK = 64
COLS = 128
RHS = 16
LEAF = 64
BLK_MUL = 1
LOCAL_SRC = 3
LOCAL_TGT = 3
LS = 2
LT = 3
NLEV = 11
BLK = 32
SLOTS = 1024
SOURCES = 65536
N_SRC = 4
N_TGT = 8


def block_scale(key, shape, split, low, top_value):
    level = 1.0
    for axis_at, blocks in split:
        heights = jax.random.uniform(jax.random.fold_in(jax.random.fold_in(key, 6), axis_at), (blocks,), jnp.float32, low / len(split), top_value / len(split))
        level = level * jnp.repeat(jnp.exp(heights), shape[axis_at] // blocks).reshape((-1,) + (1,) * (len(shape) - 1 - axis_at))
    return level


def noise(rng, shape, scale, limit, split=(), dtype=jnp.bfloat16):
    factor_of = block_scale(rng, shape, split, -0.22, 0.18) if split else 1.0
    values = jax.random.normal(rng, shape, jnp.float32) * scale * factor_of
    return jnp.minimum(jnp.maximum(values, -limit), limit).astype(dtype)


def setup_inputs(seed: int = 0) -> dict:
    splits = jax.random.split(jax.random.key(seed), 11)
    source_values = noise(splits[0], (RHS, SOURCES), 1.0, 6.0, ((1, 32),), jnp.float32)
    source_phase = jnp.clip(jax.random.uniform(splits[1], (SOURCES,), jnp.float32, -3.140625, 3.140625), -3.140625, 3.140625)
    leaf_interp = noise(splits[2], (LEAF, RANK), LEAF ** -0.5, 0.75)
    level_interp = noise(splits[3], (NLEV, 2, RANK, RANK), (2 * RANK) ** -0.5, 0.5)
    level_phase = jnp.clip(jax.random.uniform(splits[4], (NLEV, 3, SLOTS, RANK), jnp.float32, -3.140625, 3.140625), -3.140625, 3.140625)
    middle_interp = noise(splits[5], (RANK, RANK), RANK ** -0.5, 0.75)
    middle_phase = jnp.clip(jax.random.uniform(splits[6], (2, SLOTS, RANK), jnp.float32, -3.140625, 3.140625), -3.140625, 3.140625)
    final_phase = jnp.clip(jax.random.uniform(splits[7], (SLOTS, RANK), jnp.float32, -3.140625, 3.140625), -3.140625, 3.140625)
    final_interp = noise(splits[8], (RANK, LEAF), RANK ** -0.5, 0.75)
    target_phase = jnp.clip(jax.random.uniform(splits[9], (SOURCES,), jnp.float32, -3.140625, 3.140625), -3.140625, 3.140625)
    return {"source_values": source_values, "source_phase": source_phase, "leaf_interp": leaf_interp, "level_interp": level_interp, "level_phase": level_phase, "middle_interp": middle_interp, "middle_phase": middle_phase, "final_phase": final_phase, "final_interp": final_interp, "target_phase": target_phase}


def rotate(vectors, angles):
    half_width = angles.shape[-1]
    values = vectors.astype(jnp.float32)
    real_part = values[..., :half_width]
    imag_part = values[..., half_width:]
    cosine = jnp.cos(angles)[:, None, :]
    sine_val = jnp.sin(angles)[:, None, :]
    return jnp.concatenate([real_part * cosine - imag_part * sine_val, real_part * sine_val + imag_part * cosine], -1)


def block_pair(matrix):
    zeros_block = jnp.zeros_like(matrix)
    upper_rows = jnp.concatenate([matrix, zeros_block], 1)
    lower_rows = jnp.concatenate([zeros_block, matrix], 1)
    return jnp.concatenate([upper_rows, lower_rows], 0)


def flip_pairs(coeffs, stride):
    shape = coeffs.shape
    return coeffs.reshape((shape[0] // (2 * stride), 2, stride) + shape[1:])[:, ::-1].reshape(shape)


def translate(coeffs, partner, phases, matrices):
    shape = coeffs.shape
    own_rot = rotate(coeffs, phases[0]).astype(jnp.bfloat16).reshape(-1, shape[2])
    other_rot = rotate(partner, phases[1]).astype(jnp.bfloat16).reshape(-1, shape[2])
    summed = jnp.dot(own_rot, block_pair(matrices[0]), preferred_element_type=jnp.float32)
    summed = summed + jnp.dot(other_rot, block_pair(matrices[1]), preferred_element_type=jnp.float32)
    return rotate(summed.reshape(shape), phases[2]).astype(jnp.bfloat16)


def reference(source_values, source_phase, leaf_interp, level_interp, level_phase, middle_interp, middle_phase, final_phase, final_interp, target_phase):
    cos_src = jnp.cos(source_phase)[None, :]
    sin_src = jnp.sin(source_phase)[None, :]
    modulated = jnp.stack([source_values * cos_src, -source_values * sin_src]).astype(jnp.bfloat16)
    leaf_terms = jnp.dot(modulated.reshape(-1, LEAF), leaf_interp, preferred_element_type=jnp.float32)
    leaf_terms = leaf_terms.reshape(2, RHS, SLOTS, RANK).transpose(2, 1, 0, 3)
    coeffs = leaf_terms.reshape(SLOTS, RHS, COLS).astype(jnp.bfloat16)
    level_index = 0
    for step_index in range(LOCAL_SRC):
        partner = flip_pairs(coeffs, 2 ** step_index)
        coeffs = translate(coeffs, partner, level_phase[level_index], level_interp[level_index])
        level_index += 1
    for step_index in range(LS):
        partner = flip_pairs(coeffs, (SLOTS // N_SRC) * 2 ** step_index)
        coeffs = translate(coeffs, partner, level_phase[level_index], level_interp[level_index])
        level_index += 1
    devices = N_SRC * N_TGT
    regrouped = coeffs.reshape(devices, devices, BLK_MUL, RHS, COLS).transpose(1, 0, 2, 3, 4).reshape(SLOTS, RHS, COLS)
    switched = rotate(regrouped, middle_phase[0]).astype(jnp.bfloat16).reshape(-1, COLS)
    middle_sum = jnp.dot(switched, block_pair(middle_interp), preferred_element_type=jnp.float32)
    coeffs = rotate(middle_sum.reshape(SLOTS, RHS, COLS), middle_phase[1]).astype(jnp.bfloat16)
    for step_index in range(LT):
        partner = flip_pairs(coeffs, BLK * 2 ** step_index)
        coeffs = translate(coeffs, partner, level_phase[level_index], level_interp[level_index])
        level_index += 1
    for step_index in range(LOCAL_TGT):
        partner = flip_pairs(coeffs, 2 ** step_index)
        coeffs = translate(coeffs, partner, level_phase[level_index], level_interp[level_index])
        level_index += 1
    finals = rotate(coeffs, final_phase).astype(jnp.bfloat16)
    finals = finals.reshape(SLOTS, RHS, 2, RANK).transpose(2, 1, 0, 3).reshape(-1, RANK)
    evaluated = jnp.dot(finals, final_interp, preferred_element_type=jnp.float32).reshape(2, RHS, SOURCES)
    cos_tgt = jnp.cos(target_phase)[None, :]
    sin_tgt = jnp.sin(target_phase)[None, :]
    real_out = evaluated[0] * cos_tgt - evaluated[1] * sin_tgt
    imag_out = evaluated[0] * sin_tgt + evaluated[1] * cos_tgt
    return jnp.stack([real_out, imag_out])
```

```python
import functools

import jax
import jax.numpy as jnp
from jax import lax
from jax.experimental import pallas as pl
from jax.experimental.pallas import tpu as pltpu
from jax.sharding import PartitionSpec as P

LOCAL_SRC = 3
LOCAL_TGT = 3
MESH = pl.DeviceIdType.MESH
F32 = jnp.float32
BF16 = jnp.bfloat16

PI_HI = 3.140625
PI_LO = 9.67653589793e-4
SIN_C = (2.605166276178326e-06, -0.00019809046357444052, 0.008333050617328575, -0.16666657969904702, 0.9999999957158396)
COS_C = (-2.605107617861078e-07, 2.4760135505794177e-05, -0.0013888360842290288, 0.04166663620890442, -0.49999999356955516, 0.9999999997799034)


def cos_sin(x):
    k = lax.round(x * (1.0 / 3.141592653589793), lax.RoundingMethod.TO_NEAREST_EVEN)
    r = (x - k * PI_HI) - k * PI_LO
    z = r * r
    c = jnp.full_like(z, COS_C[0])
    for a in COS_C[1:]:
        c = c * z + a
    s = jnp.full_like(z, SIN_C[0])
    for a in SIN_C[1:]:
        s = s * z + a
    s = s * r
    half = k * 0.5
    odd = jnp.abs(half - lax.round(half, lax.RoundingMethod.TO_NEAREST_EVEN))
    sign = 1.0 - 4.0 * odd
    return c * sign, s * sign


def lane_low(shape, half):
    return lax.broadcasted_iota(jnp.int32, shape, len(shape) - 1) < half


def dup(x):
    return jnp.concatenate([x, x], -1)


def dup_halves(x, half):
    y = pltpu.roll(x, half, x.ndim - 1)
    low = lane_low(x.shape, half)
    return jnp.where(low, x, y), jnp.where(low, y, x)


def xor_rows(x, h):
    rows = x.shape[0]
    up = pltpu.roll(x, rows - h, 0)
    down = pltpu.roll(x, h, 0)
    row = lax.broadcasted_iota(jnp.int32, x.shape, 0)
    return jnp.where((row // h) % 2 == 0, up, down)


def xor_lead(x, h):
    return jnp.concatenate([x[i ^ h : (i ^ h) + 1] for i in range(x.shape[0])], 0)


def kernel(
    S, T, levels, src_bits, tgt_bits,
    values, sphase, leaf, lint, lphase, mint, mphase, fphase, fint, tphase,
    out,
    w, wl, wm, wf, tc, ts, ph_src, pk2, pk, ph_tgt, send1, recv1, xa, xb, send2, recv2,
    ps_send, ps_recv, pt_send, pt_recv, c1_send, c1_recv, c2_send, c2_recv,
):
    s_me = lax.axis_index("src")
    t_me = lax.axis_index("tgt")
    half = leaf.shape[1]
    R = S * T
    rhs = values.shape[0]
    rows = T * rhs
    K = LOCAL_SRC + src_bits
    M = K + tgt_bits
    N = levels

    barrier = pltpu.get_barrier_semaphore()
    for j in range(1, S):
        pl.semaphore_signal(barrier, inc=1, device_id=(lax.rem(s_me + j, S), t_me), device_id_type=MESH)
    for j in range(1, T):
        pl.semaphore_signal(barrier, inc=1, device_id=(s_me, lax.rem(t_me + j, T)), device_id_type=MESH)

    def arr(q):
        if q < 2:
            return mphase[q]
        return lphase[K + (q - 2) // 3, (q - 2) % 3]

    nq = 2 + 3 * tgt_bits
    Q = (nq + 1) // 2
    RP = pk.shape[0] // T
    for q in range(Q):
        a = arr(2 * q)
        b = arr(2 * q + 1) if 2 * q + 1 < nq else a
        pk2[q * R : (q + 1) * R, :] = jnp.concatenate([a, b], -1)
    for d in range(T):
        pk[d * RP : d * RP + Q * S, :] = pk2[pl.ds(d, Q * S, stride=T), :]

    sgn = jnp.where(lane_low((R, 2 * half), half), -1.0, 1.0)

    def put(idx, angle):
        c, s = cos_sin(angle * sgn)
        tc[idx] = c
        ts[idx] = s

    def put_level(n, prev, own, other, h):
        oth = xor_rows(other, h)
        put(2 * n, own if prev is None else prev + own)
        put(2 * n + 1, oth if prev is None else prev + oth)

    def lp(n, q):
        return dup(lphase[n, q])

    I_SEND1, I_MID, I_SEND2, I_FIN, I_TGT, I_SRC = (2 * N + i for i in range(6))

    low16 = lane_low((sphase.shape[0], 2 * half), half)

    def point_rows(ref):
        lo, hi = dup_halves(ref[...], half)
        n = lo.shape[0]
        return jnp.concatenate([jnp.concatenate([lo[i : i + 1], hi[i : i + 1]], 0) for i in range(n)], 0)

    c, s = cos_sin(point_rows(sphase))
    tc[I_SRC] = jnp.where(lane_low(c.shape, half), c, -s)
    for n in range(LOCAL_SRC):
        put_level(n, None if n == 0 else lp(n - 1, 2), lp(n, 0), lp(n, 1), 2**n)
    put(I_SEND1, lp(LOCAL_SRC - 1, 2))

    def fill(dst, r, L):
        z = jnp.zeros_like(L)
        lz = jnp.concatenate([L, z], 1)
        zl = jnp.concatenate([z, L], 1)
        wd = 2 * half
        dst[r : r + half, 0:wd] = lz
        dst[r : r + half, wd : 2 * wd] = zl
        dst[r + half : r + wd, 0:wd] = zl
        dst[r + half : r + wd, wd : 2 * wd] = lz

    fill(wl, 0, leaf[...])
    for n in range(LOCAL_SRC):
        fill(w.at[n], 0, lint[n, 0])
        fill(w.at[n], 2 * half, lint[n, 1])

    pl.semaphore_wait(barrier, S - 1 + T - 1)

    def blk(i):
        return pl.ds(pl.multiple_of(i * T, T), T)

    def ps_copy(j):
        e = lax.rem(s_me + j, S)
        return pltpu.make_async_remote_copy(
            src_ref=lphase.at[pl.ds(LOCAL_SRC, src_bits), :, blk(e), :],
            dst_ref=ph_src.at[:, :, blk(s_me), :],
            send_sem=ps_send.at[j], recv_sem=ps_recv.at[j],
            device_id=(e, t_me), device_id_type=MESH,
        )

    def pt_copy(j):
        e = lax.rem(t_me + j, T)
        return pltpu.make_async_remote_copy(
            src_ref=pk.at[pl.ds(pl.multiple_of(e * RP, 8), RP), :],
            dst_ref=ph_tgt.at[pl.ds(pl.multiple_of(t_me * RP, 8), RP), :],
            send_sem=pt_send.at[j], recv_sem=pt_recv.at[j],
            device_id=(s_me, e), device_id_type=MESH,
        )

    for j in range(1, S):
        ps_copy(j).start()
    for j in range(1, T):
        pt_copy(j).start()

    def tab(idx, i):
        return tc[idx, blk(i), :][:, None, :], ts[idx, blk(i), :][:, None, :]

    wd = 2 * half

    def split(y):
        y = y.reshape(T, rhs, 2 * wd)
        return y[:, :, :wd], y[:, :, wd:]

    def rot(v, sw, idx, i):
        c, s = tab(idx, i)
        return v * c + sw * s

    def dot(x, m):
        return jnp.dot(x, m, preferred_element_type=F32)

    def step(v, sw, n, i, h):
        own = rot(v, sw, 2 * n, i).astype(BF16)
        oth = xor_lead(rot(v, sw, 2 * n + 1, i), h).astype(BF16)
        x = jnp.concatenate([own, oth], -1).reshape(rows, 2 * wd)
        return split(dot(x, w[n]))

    def c1_copy(j):
        e = lax.rem(s_me + j, S)
        return pltpu.make_async_remote_copy(
            src_ref=send1.at[e], dst_ref=recv1.at[s_me],
            send_sem=c1_send.at[j], recv_sem=c1_recv.at[j],
            device_id=(e, t_me), device_id_type=MESH,
        )

    for j in range(1, S + 1):
        e = lax.rem(s_me + j, S)
        span = T * half
        vals = values[:, pl.ds(pl.multiple_of(e * span, span), span)]
        parts = []
        for p in range(T // 2):
            parts.extend(dup_halves(vals[:, p * wd : (p + 1) * wd], half))
        x = jnp.stack(parts, 0) * tc[I_SRC, blk(e), :][:, None, :]
        v, sw = split(dot(x.astype(BF16).reshape(rows, wd), wl[...]))
        for n in range(LOCAL_SRC):
            v, sw = step(v, sw, n, e, 2**n)
        res = rot(v, sw, I_SEND1, e).astype(BF16)
        if j < S:
            send1[e] = res
            c1_copy(j).start()
        else:
            recv1[s_me] = res

    for n in range(LOCAL_SRC, N):
        fill(w.at[n], 0, lint[n, 0])
        fill(w.at[n], 2 * half, lint[n, 1])
    fill(wm, 0, mint[...])
    fill(wf, 0, fint[...])

    ph_src[:, :, blk(s_me), :] = lphase[LOCAL_SRC:K, :, blk(s_me), :]
    own_rows = pl.ds(pl.multiple_of(t_me * RP, 8), RP)
    ph_tgt[own_rows, :] = pk[own_rows, :]

    for n in range(M, N):
        put_level(n, None if n == M else lp(n - 1, 2), lp(n, 0), lp(n, 1), 2 ** (n - M))
    put(I_FIN, lp(N - 1, 2) + dup(fphase[...]))
    put(I_TGT, point_rows(tphase))

    for j in range(1, S):
        ps_copy(j).wait()
    for b in range(src_bits):
        n = LOCAL_SRC + b
        prev = None if b == 0 else dup(ph_src[b - 1, 2])
        put_level(n, prev, dup(ph_src[b, 0]), dup(ph_src[b, 1]), T * 2**b)

    for j in range(1, T):
        pt_copy(j).wait()
    ang = []
    for q in range(Q):
        packed = jnp.concatenate(
            [ph_tgt[pl.ds(q * S + i, T, stride=RP), :] for i in range(S)], 0
        )
        ang.extend(dup_halves(packed, half))
    put(I_MID, dup(ph_src[src_bits - 1, 2]) + ang[0])
    for b in range(tgt_bits):
        n = K + b
        prev = ang[1] if b == 0 else ang[2 + 3 * (b - 1) + 2]
        put_level(n, prev, ang[2 + 3 * b], ang[2 + 3 * b + 1], 2**b)
    put(I_SEND2, ang[2 + 3 * (tgt_bits - 1) + 2])

    for j in range(1, S):
        c1_copy(j).wait()

    bufs = (xa, xb)
    for b in range(src_bits):
        n = LOCAL_SRC + b
        dst = bufs[b % 2]
        for i in range(S):
            if b == 0:
                v = recv1[i].astype(F32)
                sw = pltpu.roll(v, half, 2)
            else:
                v, sw = split(dot(bufs[(b - 1) % 2][i], w[n - 1]))
            own = rot(v, sw, 2 * n, i).astype(BF16)
            oth = rot(v, sw, 2 * n + 1, i).astype(BF16)
            dst[i, :, :wd] = own.reshape(rows, wd)
            dst[i ^ 2**b, :, wd:] = oth.reshape(rows, wd)

    def c2_copy(i, j):
        e = lax.rem(t_me + j, T)
        return pltpu.make_async_remote_copy(
            src_ref=send2.at[i, e], dst_ref=recv2.at[i, t_me],
            send_sem=c2_send.at[i, j], recv_sem=c2_recv.at[i, j],
            device_id=(s_me, e), device_id_type=MESH,
        )

    for i in range(S):
        v, sw = split(dot(bufs[(src_bits - 1) % 2][i], w[K - 1]))
        x = rot(v, sw, I_MID, i).astype(BF16).reshape(rows, wd)
        v, sw = split(dot(x, wm[...]))
        for b in range(tgt_bits):
            v, sw = step(v, sw, K + b, i, 2**b)
        send2[i] = rot(v, sw, I_SEND2, i).astype(BF16)
        for j in range(1, T):
            c2_copy(i, j).start()
        recv2[i, t_me] = send2[i, t_me]

    low3 = lane_low((rhs, wd), half)
    for i in range(S):
        for j in range(1, T):
            c2_copy(i, j).wait()
        v = recv2[i].astype(F32)
        sw = pltpu.roll(v, half, 2)
        for n in range(M, N):
            v, sw = step(v, sw, n, i, 2 ** (n - M))
        x = rot(v, sw, I_FIN, i).astype(BF16).reshape(rows, wd)
        v, sw = split(dot(x, wf[...]))
        r = rot(v, sw, I_TGT, i)
        rr = pltpu.roll(r, half, 2)
        for p in range(T // 2):
            col = pl.ds(i * T * half + p * wd, wd)
            out[0, :, col] = jnp.where(low3, r[2 * p], rr[2 * p + 1])
            out[1, :, col] = jnp.where(low3, rr[2 * p], r[2 * p + 1])


def shards(
    source_values, source_phase, leaf_interp, level_interp, level_phase,
    middle_interp, middle_phase, final_phase, final_interp, target_phase,
):
    S = lax.axis_size("src")
    T = lax.axis_size("tgt")
    R = level_phase.shape[2]
    assert R == S * T
    rhs = source_values.shape[0]
    half = leaf_interp.shape[1]
    wd = 2 * half
    N = level_phase.shape[0]
    src_bits = S.bit_length() - 1
    tgt_bits = T.bit_length() - 1
    assert N == LOCAL_SRC + src_bits + tgt_bits + LOCAL_TGT
    Q = (2 + 3 * tgt_bits + 1) // 2
    RP = -(-Q * S // 8) * 8
    ntab = 2 * N + 6
    vm = pltpu.VMEM
    dma = pltpu.SemaphoreType.DMA
    return pl.pallas_call(
        functools.partial(kernel, S, T, N, src_bits, tgt_bits),
        out_shape=jax.ShapeDtypeStruct((2,) + source_values.shape, F32),
        in_specs=[pl.BlockSpec(memory_space=pltpu.VMEM)] * 10,
        out_specs=pl.BlockSpec(memory_space=pltpu.VMEM),
        scratch_shapes=[
            vm((N, 2 * wd, 2 * wd), BF16), vm((wd, 2 * wd), BF16),
            vm((wd, 2 * wd), BF16), vm((wd, 2 * wd), BF16),
            vm((ntab, R, wd), F32), vm((ntab, R, wd), F32),
            vm((src_bits, 3, R, half), F32), vm((Q * R, wd), F32),
            vm((T * RP, wd), F32), vm((T * RP, wd), F32),
            vm((S, T, rhs, wd), BF16), vm((S, T, rhs, wd), BF16),
            vm((S, T * rhs, 2 * wd), BF16), vm((S, T * rhs, 2 * wd), BF16),
            vm((S, T, rhs, wd), BF16), vm((S, T, rhs, wd), BF16),
            dma((S,)), dma((S,)), dma((T,)), dma((T,)),
            dma((S,)), dma((S,)), dma((S, T)), dma((S, T)),
        ],
        compiler_params=pltpu.CompilerParams(collective_id=0, has_side_effects=True),
    )(
        source_values, source_phase.reshape(-1, wd), leaf_interp, level_interp, level_phase,
        middle_interp, middle_phase, final_phase, final_interp, target_phase.reshape(-1, wd),
    )


def solution(mesh):
    return jax.shard_map(
        shards,
        mesh=mesh,
        in_specs=(
            P(None, ("src", "tgt")),
            P(("src", "tgt")),
            P(),
            P(),
            P(None, None, ("src", "tgt"), None),
            P(),
            P(None, ("src", "tgt"), None),
            P(("src", "tgt"), None),
            P(),
            P(("src", "tgt")),
        ),
        out_specs=P(None, None, ("src", "tgt")),
        check_vma=False,
    )
```

```python
import functools

import jax
import jax.numpy as jnp
from jax import lax
from jax.experimental import pallas as pl
from jax.experimental.pallas import tpu as pltpu
from jax.sharding import PartitionSpec as P

LOCAL_SRC = 3
LOCAL_TGT = 3
MESH = pl.DeviceIdType.MESH
GROUP = 2
VLIM = 67043328
F32 = jnp.float32
BF16 = jnp.bfloat16

PI_HI = 3.140625
PI_LO = 9.67653589793e-4
SIN_C = (2.605166276178326e-06, -0.00019809046357444052, 0.008333050617328575, -0.16666657969904702, 0.9999999957158396)
COS_C = (-2.605107617861078e-07, 2.4760135505794177e-05, -0.0013888360842290288, 0.04166663620890442, -0.49999999356955516, 0.9999999997799034)


def cos_sin(x):
    k = lax.round(x * (1.0 / 3.141592653589793), lax.RoundingMethod.TO_NEAREST_EVEN)
    r = (x - k * PI_HI) - k * PI_LO
    z = r * r
    c = jnp.full_like(z, COS_C[0])
    for a in COS_C[1:]:
        c = c * z + a
    s = jnp.full_like(z, SIN_C[0])
    for a in SIN_C[1:]:
        s = s * z + a
    s = s * r
    half = k * 0.5
    odd = jnp.abs(half - lax.round(half, lax.RoundingMethod.TO_NEAREST_EVEN))
    sign = 1.0 - 4.0 * odd
    return c * sign, s * sign


def lane_low(shape, half):
    return lax.broadcasted_iota(jnp.int32, shape, len(shape) - 1) < half


def dup(x):
    return jnp.concatenate([x, x], -1)


def dup_halves(x, half):
    y = pltpu.roll(x, half, x.ndim - 1)
    low = lane_low(x.shape, half)
    return jnp.where(low, x, y), jnp.where(low, y, x)


def xor_rows(x, h):
    rows = x.shape[0]
    up = pltpu.roll(x, rows - h, 0)
    down = pltpu.roll(x, h, 0)
    row = lax.broadcasted_iota(jnp.int32, x.shape, 0)
    return jnp.where((row // h) % 2 == 0, up, down)


def xor_lead(x, h):
    return jnp.concatenate([x[i ^ h : (i ^ h) + 1] for i in range(x.shape[0])], 0)


def xor_index(i, j, size):
    bit = 1
    res = i
    while bit < size:
        if j & bit:
            res = res + bit * (1 - 2 * lax.rem(i // bit, 2))
        bit *= 2
    return res


def kernel(
    S, T, levels, src_bits, tgt_bits,
    values_h, sphase_h, leaf_h, lint_h, lphase_h, mint_h, mphase_h, fphase_h, fint_h, tphase_h,
    out,
    values, sphase, leaf, lint, lphase, mint, mphase, fphase, fint, tphase, obuf, in_sem, out_sem,
    w, wl, wm, wf, tc, ts, ph_src, pk2, pk, ph_tgt, send1, recv1, xa, xb, send2, recv2,
    ps_send, ps_recv, pt_send, pt_recv, c1_send, c1_recv, c2_send, c2_recv,
):
    s_me = lax.axis_index("src")
    t_me = lax.axis_index("tgt")
    half = leaf.shape[1]
    span = T * half
    R = S * T
    rhs = values.shape[0]
    rows = T * rhs
    K = LOCAL_SRC + src_bits
    M = K + tgt_bits
    N = levels

    barrier = pltpu.get_barrier_semaphore()
    for j in range(1, S):
        pl.semaphore_signal(barrier, inc=1, device_id=(lax.rem(s_me + j, S), t_me), device_id_type=MESH)
    for j in range(1, T):
        pl.semaphore_signal(barrier, inc=1, device_id=(s_me, lax.rem(t_me + j, T)), device_id_type=MESH)

    loads = [
        pltpu.make_async_copy(a, b, in_sem.at[i])
        for i, (a, b) in enumerate(
            (
                (sphase_h, sphase), (lphase_h, lphase), (leaf_h, leaf), (values_h, values),
                (lint_h, lint), (mphase_h, mphase), (fphase_h, fphase), (tphase_h, tphase),
                (mint_h, mint), (fint_h, fint),
            )
        )
    ]
    for load in loads:
        load.start()
    for load in loads[:3]:
        load.wait()

    sgn = jnp.where(lane_low((R, 2 * half), half), -1.0, 1.0)

    def put(idx, angle):
        c, s = cos_sin(angle * sgn)
        tc[idx] = c
        ts[idx] = s

    def put_level(n, prev, own, other, h):
        oth = xor_rows(other, h)
        put(2 * n, own if prev is None else prev + own)
        put(2 * n + 1, oth if prev is None else prev + oth)

    def lp(n, q):
        return dup(lphase[n, q])

    I_SEND1, I_MID, I_SEND2, I_FIN, I_TGT, I_SRC = (2 * N + i for i in range(6))

    low16 = lane_low((sphase.shape[0], 2 * half), half)

    def point_rows(ref):
        lo, hi = dup_halves(ref[...], half)
        n = lo.shape[0]
        return jnp.concatenate([jnp.concatenate([lo[i : i + 1], hi[i : i + 1]], 0) for i in range(n)], 0)

    c, s = cos_sin(point_rows(sphase))
    tc[I_SRC] = jnp.where(lane_low(c.shape, half), c, -s)
    for n in range(LOCAL_SRC):
        put_level(n, None if n == 0 else lp(n - 1, 2), lp(n, 0), lp(n, 1), 2**n)
    put(I_SEND1, lp(LOCAL_SRC - 1, 2))

    def fill(dst, r, L):
        z = jnp.zeros_like(L)
        lz = jnp.concatenate([L, z], 1)
        zl = jnp.concatenate([z, L], 1)
        wd = 2 * half
        dst[r : r + half, 0:wd] = lz
        dst[r : r + half, wd : 2 * wd] = zl
        dst[r + half : r + wd, 0:wd] = zl
        dst[r + half : r + wd, wd : 2 * wd] = lz

    fill(wl, 0, leaf[...])
    loads[4].wait()
    for n in range(LOCAL_SRC):
        fill(w.at[n], 0, lint[n, 0])
        fill(w.at[n], 2 * half, lint[n, 1])

    def blk(i):
        return pl.ds(pl.multiple_of(i * T, T), T)

    def ps_copy(j):
        e = xor_index(s_me, j, S)
        return pltpu.make_async_remote_copy(
            src_ref=lphase.at[pl.ds(LOCAL_SRC, src_bits), :, blk(e), :],
            dst_ref=ph_src.at[:, :, blk(s_me), :],
            send_sem=ps_send.at[j], recv_sem=ps_recv.at[j],
            device_id=(e, t_me), device_id_type=MESH,
        )

    def pt_copy(j):
        e = xor_index(t_me, j, T)
        return pltpu.make_async_remote_copy(
            src_ref=pk.at[pl.ds(pl.multiple_of(e * RP, 8), RP), :],
            dst_ref=ph_tgt.at[pl.ds(pl.multiple_of(t_me * RP, 8), RP), :],
            send_sem=pt_send.at[j], recv_sem=pt_recv.at[j],
            device_id=(s_me, e), device_id_type=MESH,
        )

    def tab(idx, i):
        return tc[idx, blk(i), :][:, None, :], ts[idx, blk(i), :][:, None, :]

    wd = 2 * half

    def split(y):
        y = y.reshape(T, rhs, 2 * wd)
        return y[:, :, :wd], y[:, :, wd:]

    def rot(v, sw, idx, i):
        c, s = tab(idx, i)
        return v * c + sw * s

    def dot(x, m):
        return jnp.dot(x, m, preferred_element_type=F32)

    def step(v, sw, n, i, h):
        own = rot(v, sw, 2 * n, i).astype(BF16)
        oth = xor_lead(rot(v, sw, 2 * n + 1, i), h).astype(BF16)
        x = jnp.concatenate([own, oth], -1).reshape(rows, 2 * wd)
        return split(dot(x, w[n]))

    def c1_copy(j):
        e = xor_index(s_me, j, S)
        return pltpu.make_async_remote_copy(
            src_ref=send1.at[e], dst_ref=recv1.at[s_me],
            send_sem=c1_send.at[j], recv_sem=c1_recv.at[j],
            device_id=(e, t_me), device_id_type=MESH,
        )

    loads[3].wait()
    state = []
    for e in range(S):
        parts = []
        for p in range(T // 2):
            parts.extend(dup_halves(values[:, e * span + p * wd : e * span + (p + 1) * wd], half))
        x = jnp.stack(parts, 0) * tc[I_SRC, blk(e), :][:, None, :]
        state.append(split(dot(x.astype(BF16).reshape(rows, wd), wl[...])))
    for n in range(LOCAL_SRC):
        state = [step(v, sw, n, e, 2**n) for e, (v, sw) in enumerate(state)]
    for e, (v, sw) in enumerate(state):
        send1[e] = rot(v, sw, I_SEND1, e).astype(BF16)

    loads[5].wait()
    def arr(q):
        if q < 2:
            return mphase[q]
        return lphase[K + (q - 2) // 3, (q - 2) % 3]

    nq = 2 + 3 * tgt_bits
    Q = (nq + 1) // 2
    RP = pk.shape[0] // T
    for q in range(Q):
        a = arr(2 * q)
        b = arr(2 * q + 1) if 2 * q + 1 < nq else a
        pk2[q * R : (q + 1) * R, :] = jnp.concatenate([a, b], -1)
    for d in range(T):
        pk[d * RP : d * RP + Q * S, :] = pk2[pl.ds(d, Q * S, stride=T), :]

    pl.semaphore_wait(barrier, S - 1 + T - 1)
    for j in range(S - 1, 0, -1):
        ps_copy(j).start()
    for j in range(T - 1, 0, -1):
        pt_copy(j).start()

    for j in range(S - 1, 0, -1):
        c1_copy(j).start()
    recv1[s_me] = send1[s_me]

    for load in loads[6:]:
        load.wait()
    for n in range(LOCAL_SRC, N):
        fill(w.at[n], 0, lint[n, 0])
        fill(w.at[n], 2 * half, lint[n, 1])
    fill(wm, 0, mint[...])
    fill(wf, 0, fint[...])

    ph_src[:, :, blk(s_me), :] = lphase[LOCAL_SRC:K, :, blk(s_me), :]
    own_rows = pl.ds(pl.multiple_of(t_me * RP, 8), RP)
    ph_tgt[own_rows, :] = pk[own_rows, :]

    for n in range(M, N):
        put_level(n, None if n == M else lp(n - 1, 2), lp(n, 0), lp(n, 1), 2 ** (n - M))
    put(I_FIN, lp(N - 1, 2) + dup(fphase[...]))
    put(I_TGT, point_rows(tphase))

    for j in range(1, S):
        ps_copy(j).wait()
    for b in range(src_bits):
        n = LOCAL_SRC + b
        prev = None if b == 0 else dup(ph_src[b - 1, 2])
        put_level(n, prev, dup(ph_src[b, 0]), dup(ph_src[b, 1]), T * 2**b)

    for j in range(1, T):
        pt_copy(j).wait()
    ang = []
    for q in range(Q):
        packed = jnp.concatenate(
            [ph_tgt[pl.ds(q * S + i, T, stride=RP), :] for i in range(S)], 0
        )
        ang.extend(dup_halves(packed, half))
    put(I_MID, dup(ph_src[src_bits - 1, 2]) + ang[0])
    for b in range(tgt_bits):
        n = K + b
        prev = ang[1] if b == 0 else ang[2 + 3 * (b - 1) + 2]
        put_level(n, prev, ang[2 + 3 * b], ang[2 + 3 * b + 1], 2**b)
    put(I_SEND2, ang[2 + 3 * (tgt_bits - 1) + 2])

    for j in range(1, S):
        c1_copy(j).wait()

    bufs = (xa, xb)
    for b in range(src_bits):
        n = LOCAL_SRC + b
        dst = bufs[b % 2]
        for i in range(S):
            if b == 0:
                v = recv1[i].astype(F32)
                sw = pltpu.roll(v, half, 2)
            else:
                v, sw = split(dot(bufs[(b - 1) % 2][i], w[n - 1]))
            own = rot(v, sw, 2 * n, i).astype(BF16)
            oth = rot(v, sw, 2 * n + 1, i).astype(BF16)
            dst[i, :, :wd] = own.reshape(rows, wd)
            dst[i ^ 2**b, :, wd:] = oth.reshape(rows, wd)

    def c2_copy(i, j):
        e = xor_index(t_me, j, T)
        return pltpu.make_async_remote_copy(
            src_ref=send2.at[i, e], dst_ref=recv2.at[i, t_me],
            send_sem=c2_send.at[i, j], recv_sem=c2_recv.at[i, j],
            device_id=(s_me, e), device_id_type=MESH,
        )

    for g in range(0, S, GROUP):
        blocks = range(g, min(g + GROUP, S))
        state = [split(dot(bufs[(src_bits - 1) % 2][i], w[K - 1])) for i in blocks]
        state = [rot(v, sw, I_MID, i).astype(BF16).reshape(rows, wd) for i, (v, sw) in zip(blocks, state)]
        state = [split(dot(x, wm[...])) for x in state]
        for b in range(tgt_bits):
            state = [step(v, sw, K + b, i, 2**b) for i, (v, sw) in zip(blocks, state)]
        for i, (v, sw) in zip(blocks, state):
            send2[i] = rot(v, sw, I_SEND2, i).astype(BF16)
        for i in blocks:
            for j in range(T - 1, 0, -1):
                c2_copy(i, j).start()
            recv2[i, t_me] = send2[i, t_me]

    low3 = lane_low((rhs, wd), half)

    def o_copy(i):
        cols = pl.ds(i * span, span)
        return pltpu.make_async_copy(obuf.at[:, :, cols], out.at[:, :, cols], out_sem.at[i])

    for g in range(0, S, GROUP):
        blocks = range(g, min(g + GROUP, S))
        for i in blocks:
            for j in range(1, T):
                c2_copy(i, j).wait()
        state = []
        for i in blocks:
            v = recv2[i].astype(F32)
            state.append((v, pltpu.roll(v, half, 2)))
        for n in range(M, N):
            state = [step(v, sw, n, i, 2 ** (n - M)) for i, (v, sw) in zip(blocks, state)]
        state = [rot(v, sw, I_FIN, i).astype(BF16).reshape(rows, wd) for i, (v, sw) in zip(blocks, state)]
        state = [split(dot(x, wf[...])) for x in state]
        for i, (v, sw) in zip(blocks, state):
            r = rot(v, sw, I_TGT, i)
            rr = pltpu.roll(r, half, 2)
            for p in range(T // 2):
                col = pl.ds(i * T * half + p * wd, wd)
                obuf[0, :, col] = jnp.where(low3, r[2 * p], rr[2 * p + 1])
                obuf[1, :, col] = jnp.where(low3, rr[2 * p], r[2 * p + 1])
            o_copy(i).start()
    for i in range(S):
        o_copy(i).wait()


def shards(
    source_values, source_phase, leaf_interp, level_interp, level_phase,
    middle_interp, middle_phase, final_phase, final_interp, target_phase,
):
    S = lax.axis_size("src")
    T = lax.axis_size("tgt")
    R = level_phase.shape[2]
    assert R == S * T
    rhs = source_values.shape[0]
    half = leaf_interp.shape[1]
    wd = 2 * half
    N = level_phase.shape[0]
    src_bits = S.bit_length() - 1
    tgt_bits = T.bit_length() - 1
    assert N == LOCAL_SRC + src_bits + tgt_bits + LOCAL_TGT
    Q = (2 + 3 * tgt_bits + 1) // 2
    RP = -(-Q * S // 8) * 8
    ntab = 2 * N + 6
    vm = pltpu.VMEM
    dma = pltpu.SemaphoreType.DMA
    args = (
        source_values, source_phase.reshape(-1, wd), leaf_interp, level_interp, level_phase,
        middle_interp, middle_phase, final_phase, final_interp, target_phase.reshape(-1, wd),
    )
    return pl.pallas_call(
        functools.partial(kernel, S, T, N, src_bits, tgt_bits),
        out_shape=jax.ShapeDtypeStruct((2,) + source_values.shape, F32),
        in_specs=[pl.BlockSpec(memory_space=pltpu.HBM)] * 10,
        out_specs=pl.BlockSpec(memory_space=pl.ANY),
        scratch_shapes=[vm(a.shape, a.dtype) for a in args] + [
            vm((2,) + source_values.shape, F32), dma((10,)), dma((S,)),
            vm((N, 2 * wd, 2 * wd), BF16), vm((wd, 2 * wd), BF16),
            vm((wd, 2 * wd), BF16), vm((wd, 2 * wd), BF16),
            vm((ntab, R, wd), F32), vm((ntab, R, wd), F32),
            vm((src_bits, 3, R, half), F32), vm((Q * R, wd), F32),
            vm((T * RP, wd), F32), vm((T * RP, wd), F32),
            vm((S, T, rhs, wd), BF16), vm((S, T, rhs, wd), BF16),
            vm((S, T * rhs, 2 * wd), BF16), vm((S, T * rhs, 2 * wd), BF16),
            vm((S, T, rhs, wd), BF16), vm((S, T, rhs, wd), BF16),
            dma((S,)), dma((S,)), dma((T,)), dma((T,)),
            dma((S,)), dma((S,)), dma((S, T)), dma((S, T)),
        ],
        compiler_params=pltpu.CompilerParams(
            collective_id=0, has_side_effects=True, vmem_limit_bytes=VLIM
        ),
    )(*args)


def solution(mesh):
    return jax.shard_map(
        shards,
        mesh=mesh,
        in_specs=(
            P(None, ("src", "tgt")),
            P(("src", "tgt")),
            P(),
            P(),
            P(None, None, ("src", "tgt"), None),
            P(),
            P(None, ("src", "tgt"), None),
            P(("src", "tgt"), None),
            P(),
            P(("src", "tgt")),
        ),
        out_specs=P(None, None, ("src", "tgt")),
        check_vma=False,
    )
```
